512 devices in a mesh: ctx: 16 (over y, z_hi), exp: 16 (over x, z_lo), dp: 2 (over core).
Axes of the slice: x: 4, y: 4, z: 16 (z_hi: 4, z_lo: 4; z = z_hi * 4 + z_lo), core: 2. Of those that a mesh axis runs over, the one named last changes fastest.
Arguments:
- queries: bfloat16 [32, 3072, 2048], P(('dp', 'exp'), 'ctx'), parts along dimension 0, may hold values from -38 to 38
- keys: bfloat16 [32, 3072, 256], P(('dp', 'exp'), 'ctx'), parts along dimension 0, may hold values from -4 to 4
- values: bfloat16 [32, 3072, 256], P(('dp', 'exp'), 'ctx'), parts along dimension 0, may hold values from -6 to 6
- segments: int32 [32, 3072], P(('dp', 'exp')), parts along dimension 0, may hold values from 0 to 7, never falling along the last dimension, each value on 1 to 1536 neighbouring positions
- residual: bfloat16 [32, 3072, 1024], P(('dp', 'exp'), 'ctx'), parts along dimension 0, may hold values from -3 to 3
- out_weight: bfloat16 [2048, 1024], P('ctx'), may hold values from -0.125 to 0.125
- gain: float32 [1024], replicated, may hold values from 0.1 to 1.9
- expert_ids: int32 [32, 3072, 8], P(('dp', 'exp'), 'ctx'), parts along dimension 0, may hold values from 0 to 127, all different within a row; in each aligned block of 192 rows (0 to 191, 192 to 383, ..., all dimensions but the last counted through in order) at most 24 rows name the same one
- route_weights: float32 [32, 3072, 8], P(('dp', 'exp'), 'ctx'), parts along dimension 0, may hold values from 0.05 to 0.5
- w_gate: bfloat16 [16, 1024, 384], P('exp'), may hold values from -0.1875 to 0.1875
- w_up: bfloat16 [16, 1024, 384], P('exp'), may hold values from -0.1875 to 0.1875
- w_down: bfloat16 [16, 384, 1024], P('exp'), may hold values from -0.3125 to 0.3125
Outputs:
- layer_out: bfloat16 [32, 3072, 1024], P(('dp', 'exp'), 'ctx'), parts along dimension 0
The draws below stay inside these ranges and needn't reach their ends.
There are 2 independent parts, one for each index of `dp`. The reference program is written for one: setup_inputs(seed, part) draws one part's arguments, and reference() takes and returns one part's arrays. A program takes and returns all parts, laid end to end along the dimension named above; an argument that names none is the same for every part. Nothing has to cross between parts.
Inputs may be any that keep to these rules, and one draw needn't show every extreme that they name: `expert_ids`: in every aligned block of 192 positions of a sequence (one slab), no expert is named by more than 24 tokens, and in every draw some expert is named by exactly 24 tokens of some block; a token names 8 different experts. `segments`: document numbers never fall along a sequence.
All inputs are finite; a program needn't handle non-finite values.
Results may differ from the reference program's by a relative error of at most 0.006.
Values may be sent and summed in bfloat16 or wider, within the bound.
A program may use at most 64 MiB of HBM per device.

```python
import math
import jax
import jax.numpy as jnp
import numpy as np
from jax import lax

D = 1024
HQ = 16
KVH = 2
HD = 128
FFE = 384
EXPERTS = 128
TOP = 8
DOCS = 8
TOK_DEV = 192
SEQ = 3072
SEQS = 16
EXPERTS_FL = 16
CAP = 24
N_CTX = 16


def pair_fields(key):
    query_key = jax.random.fold_in(key, 101)
    key_key = jax.random.fold_in(key, 202)
    key_field = jnp.clip(jax.random.normal(key_key, (SEQS, SEQ, KVH, HD), jnp.float32), -4.0, 4.0)
    query_field = jnp.clip(jax.random.normal(query_key, (SEQS, SEQ, HQ * HD), jnp.float32), -4.0, 4.0)
    return (query_field, key_field.reshape(SEQS, SEQ, KVH * HD))


def draw_queries(key, part):
    return pair_fields(key)[0].astype(jnp.bfloat16)


def draw_keys(key, part):
    return pair_fields(key)[1].astype(jnp.bfloat16)


def block_levels(stream_key, extent, split, least, high):
    loudness = 1.0
    for dim, blocks in split:
        steps = jax.random.uniform(jax.random.fold_in(jax.random.fold_in(stream_key, 6), dim), (blocks,), jnp.float32, least / len(split), high / len(split))
        loudness = loudness * jnp.repeat(jnp.exp(steps), extent[dim] // blocks).reshape((-1,) + (1,) * (len(extent) - 1 - dim))
    return loudness


def length_profile(count, total, bound, skew):
    loads = [(1 << 20) // math.isqrt(grade ** skew) + 1 for grade in range(2, count + 1)]
    surplus, given = total - bound - (count - 1), [1] * (count - 1)
    while surplus > 0:
        movable = [i for i in range(count - 1) if given[i] < bound]
        pool, budget = sum([loads[i] for i in movable]), surplus
        for i in movable:
            more = min(bound - given[i], max(1, budget * loads[i] // pool), surplus)
            given[i] = given[i] + more
            surplus = surplus - more
    return np.array([bound] + given)


def ragged_sizes(stream_key, amount, total, limit, skew):
    if amount == 2:
        one = jax.random.randint(stream_key, (), max(1, total - limit), min(limit, total - 1) + 1)
        return jnp.stack([one, total - one])
    sizes = jnp.asarray(length_profile(amount, total, limit, skew), jnp.int32)
    twos = (amount - 1) // 2
    donor, sink = sizes[1:1 + 2 * twos:2], sizes[2:2 + 2 * twos:2]
    slack = jnp.minimum(donor - 1, limit - sink)
    passed = jax.random.randint(jax.random.fold_in(stream_key, 1), (twos,), 0, 1 << 20) % (slack + 1)
    sizes = sizes.at[1:1 + 2 * twos:2].set(donor - passed).at[2:2 + 2 * twos:2].set(sink + passed)
    return sizes[jax.random.permutation(jax.random.fold_in(stream_key, 2), amount)]


def deal_out(rng, own, number, rows, amount, top, reach, skew):
    order = jax.random.permutation(rng, amount)
    packed, usual = shares(amount, rows * top, reach, skew, True), shares(amount, rows * top, reach, skew, False)
    places = jnp.arange(amount)

    def named(tallies, rotation):
        used = int((tallies > 0).sum())
        fixed = max(1, used // 4)
        shifted = fixed + (places - fixed + rotation * (used - fixed)) % max(1, amount - fixed)
        return jnp.zeros((amount,), jnp.int32).at[order[jnp.where(places < fixed, places, shifted)]].set(jnp.asarray(tallies, jnp.int32))

    tallies = jnp.where(number % 4 == 0, named(packed, number // 4), named(usual, number - number // 4 - 1))
    mixed = jax.random.permutation(jax.random.fold_in(own, 3), amount)
    giver, taker = mixed[0:amount // 2 * 2:2], mixed[1:amount // 2 * 2:2]
    margin = jnp.minimum(tallies[giver] - 1, reach - tallies[taker]) // 2
    margin = jnp.where((giver == order[0]) | (taker == order[0]) | (tallies[taker] == 0), 0, jnp.maximum(margin, 0))
    shifted = jax.random.randint(jax.random.fold_in(own, 4), (amount // 2,), 0, 1 << 20) % (margin + 1)
    tallies = tallies.at[giver].add(-shifted).at[taker].add(shifted)
    items = jnp.searchsorted(jnp.cumsum(tallies), jnp.arange(rows * top), side="right").astype(jnp.int32)
    listing = items.reshape(top, rows).T
    listing = listing[jax.random.permutation(jax.random.fold_in(own, 1), rows)]
    rotation = jax.random.randint(jax.random.fold_in(own, 2), (rows, 1), 0, top)
    return jnp.take_along_axis(listing, (jnp.arange(top)[None, :] + rotation) % top, axis=1)


def shares(amount, total, reach, lean, full):
    weights = [(1 << 20) // math.isqrt(grade ** lean) + 1 for grade in range(1, amount + 1)]
    largest = reach if full else min(reach, max(-(-total // amount), total * weights[0] // sum(weights)))
    least = 1 if total - largest >= amount - 1 else 0
    holding, spare = [largest] + [least] * (amount - 1), total - largest - least * (amount - 1)
    while spare > 0:
        free = [i for i in range(1, amount) if holding[i] < largest] or [i for i in range(1, amount) if holding[i] < reach]
        whole, left = sum([weights[i] for i in free]), spare
        for i in free:
            addition = min(reach - holding[i], max(1, left * weights[i] // whole), spare)
            holding[i] = holding[i] + addition
            spare = spare - addition
    return np.array(holding)


def gaussian(own_key, extent, scale, limit, pieces=(), held_as=jnp.bfloat16):
    result = scale * jax.random.normal(own_key, extent, jnp.float32)
    if pieces:
        result = result * block_levels(own_key, extent, pieces, -0.22, 0.18)
    return jnp.clip(result, -limit, limit).astype(held_as)


def setup_inputs(seed: int = 0, part: int = 0) -> dict:
    key_list = jax.random.split(jax.random.key(seed), 13)
    part_keys = jax.random.split(jax.random.fold_in(key_list[12], part), 13)
    queries = draw_queries(jax.random.fold_in(jax.random.fold_in(key_list[12], part), 71), part)
    keys = draw_keys(jax.random.fold_in(jax.random.fold_in(key_list[12], part), 71), part)
    values = gaussian(part_keys[2], (SEQS, SEQ, KVH * HD), 1.0, 6.0, ((0, 16), (1, 16)))
    segments = jax.vmap(lambda own: jnp.searchsorted(jnp.cumsum(ragged_sizes(own, DOCS, SEQ, SEQ // 2, 2)), jnp.arange(SEQ), side="right"))(jax.random.split(part_keys[3], SEQS)).reshape((SEQS, SEQ)).astype(jnp.int32)
    residual = gaussian(part_keys[4], (SEQS, SEQ, D), 0.5, 3.0, ((0, 16), (1, 16)))
    out_weight = gaussian(key_list[5], (HQ * HD, D), (HQ * HD) ** -0.5, 0.125, ((0, 16),))
    gain = jnp.clip(1.0 + 0.18 * jax.random.normal(key_list[6], (D,), jnp.float32), 0.1, 1.9)
    expert_ids_keys = jax.random.split(jax.random.fold_in(part_keys[7], 1), SEQS * SEQ // TOK_DEV)
    expert_ids_turns = jax.random.permutation(jax.random.fold_in(part_keys[7], 3), SEQS * SEQ // TOK_DEV)
    expert_ids = jax.vmap(lambda own, number: deal_out(jax.random.fold_in(part_keys[7], 2), own, number, TOK_DEV, EXPERTS, TOP, CAP, 2))(expert_ids_keys, expert_ids_turns).reshape((SEQS, SEQ, TOP))
    route_weights = jnp.clip(jnp.exp(math.log(0.5) - 2.3025851 * jax.random.uniform(part_keys[8], (SEQS, SEQ, TOP), jnp.float32) ** block_levels(part_keys[8], (SEQS, SEQ, TOP), ((0, 16), (1, 16)), -0.2, 0.2)), 0.05, 0.5)
    w_gate = gaussian(key_list[9], (EXPERTS_FL, D, FFE), D ** -0.5, 0.1875, ((0, 16),))
    w_up = gaussian(key_list[10], (EXPERTS_FL, D, FFE), D ** -0.5, 0.1875, ((0, 16),))
    w_down = gaussian(key_list[11], (EXPERTS_FL, FFE, D), FFE ** -0.5, 0.3125, ((0, 16),))
    return {"queries": queries, "keys": keys, "values": values, "segments": segments, "residual": residual, "out_weight": out_weight, "gain": gain, "expert_ids": expert_ids, "route_weights": route_weights, "w_gate": w_gate, "w_up": w_up, "w_down": w_down}


def attend_sequence(operands):
    query_seq, key_seq, value_seq, seg_seq = operands
    groups = HQ // KVH
    block = math.gcd(SEQ, 256)
    scale_factor = 1.0 / math.sqrt(HD)
    key_f32 = key_seq.astype(jnp.float32).reshape(SEQ, KVH, HD)
    value_f32 = value_seq.astype(jnp.float32).reshape(SEQ, KVH, HD)
    key_pos = jnp.arange(SEQ, dtype=jnp.int32)

    def query_block(index):
        first_row = index * block
        query_f32 = lax.dynamic_slice_in_dim(query_seq, first_row, block, 0).astype(jnp.float32).reshape(block, KVH, groups, HD)
        query_pos = first_row + jnp.arange(block, dtype=jnp.int32)
        query_seg = lax.dynamic_slice_in_dim(seg_seq, first_row, block, 0)
        scores = jnp.einsum('qkgd,skd->qkgs', query_f32, key_f32) * scale_factor
        allowed = ((key_pos[None, :] <= query_pos[:, None]) & (seg_seq[None, :] == query_seg[:, None]))[:, None, None, :]
        row_max = lax.optimization_barrier(jnp.max(jnp.where(allowed, scores, -jnp.inf), axis=-1, keepdims=True))
        expo = jnp.where(allowed, jnp.exp(scores - row_max), 0.0)
        norm_sum = lax.optimization_barrier(jnp.sum(expo, axis=-1))
        probs = lax.optimization_barrier(expo.astype(jnp.bfloat16)).astype(jnp.float32)
        mixed = jnp.einsum('qkgs,skd->qkgd', probs, value_f32) / norm_sum[..., None]
        return mixed.reshape(block, HQ * HD).astype(jnp.bfloat16)
    return lax.map(query_block, jnp.arange(SEQ // block, dtype=jnp.int32)).reshape(SEQ, HQ * HD)

def reference(queries, keys, values, segments, residual, out_weight, gain, expert_ids, route_weights, w_gate, w_up, w_down):
    attended = lax.map(attend_sequence, (queries, keys, values, segments))
    total_tok = SEQS * SEQ
    projected = jnp.dot(attended.reshape(total_tok, HQ * HD), out_weight, preferred_element_type=jnp.float32)
    hidden_state = residual.reshape(total_tok, D).astype(jnp.float32) + projected
    normed = (hidden_state * lax.rsqrt(lax.optimization_barrier(jnp.mean(hidden_state * hidden_state, axis=-1, keepdims=True)) + 1e-06) * gain).astype(jnp.bfloat16)
    flat_ids = expert_ids.reshape(total_tok * TOP)
    flat_weights = jnp.concatenate([route_weights.reshape(total_tok * TOP), jnp.zeros((1,), jnp.float32)])
    normed_pad = jnp.concatenate([normed, jnp.zeros((1, D), jnp.bfloat16)], axis=0)
    most_rows = SEQS * N_CTX * CAP

    def one_expert(running, expert):
        index_list = jnp.nonzero(flat_ids == expert, size=most_rows, fill_value=total_tok * TOP)[0].astype(jnp.int32)
        token_index = index_list // TOP
        chosen_rows = normed_pad[token_index]
        gate_part = jnp.dot(chosen_rows, w_gate[expert], preferred_element_type=jnp.float32)
        up_part = jnp.dot(chosen_rows, w_up[expert], preferred_element_type=jnp.float32)
        expert_hidden = (jax.nn.silu(gate_part) * up_part).astype(jnp.bfloat16)
        expert_out = jnp.dot(expert_hidden, w_down[expert], preferred_element_type=jnp.float32).astype(jnp.bfloat16)
        running = running.at[token_index].add(flat_weights[index_list][:, None] * expert_out.astype(jnp.float32))
        return (running, None)
    moe_sum, _ = lax.scan(one_expert, jnp.zeros((total_tok + 1, D), jnp.float32), jnp.arange(EXPERTS_FL, dtype=jnp.int32))
    layer_out = (hidden_state + moe_sum[:total_tok]).astype(jnp.bfloat16)
    return layer_out.reshape(SEQS, SEQ, D)
```

```python
import math

import jax
import jax.numpy as jnp
from jax import lax
from jax.experimental import pallas as pl
from jax.experimental.pallas import tpu as pltpu
from jax.sharding import PartitionSpec as P

HQ = 16
KVH = 2
HD = 128
TOP = 8
CAP = 24
TOK = 192
WIDTH = 1024
OWNERS = 16
SLOTS = OWNERS * CAP
PER = 4
BLOCKS = HQ // PER
LANES = PER * TOK
NEG = -1e30
MESH = pl.DeviceIdType.MESH
SCALE2 = math.log2(math.e) / math.sqrt(HD)
OWN, LEFT, RIGHT, FAR = range(4)


def attend_kernel(
    queries, segs, residual, gain, ids, weights, keys_hbm, values_hbm, w_hbm,
    hidden_out, rows_out, hi_out, lo_out,
    kbuf, vbuf, vtransit, wbuf, q_s, m_s, l_s, acc_s, start_s, qpos_s, att_s,
    send_sems, recv_sems, local_sems,
):
    c = lax.axis_index("ctx")
    e = lax.axis_index("exp")
    core = lax.axis_index("dp")
    y, h = c // 4, c % 4
    x, z = e // 4, e % 4
    zr, zl = {"ctx": y * 4 + (h + 1) % 4}, {"ctx": y * 4 + (h + 3) % 4}
    yu, yd = {"ctx": ((y + 1) % 4) * 4 + h}, {"ctx": ((y + 3) % 4) * 4 + h}
    xu, xd = {"exp": ((x + 1) % 4) * 4 + z}, {"exp": ((x + 3) % 4) * 4 + z}
    twin = {"dp": 1 - core}
    partners = (zr, zl, yu, yd, xu, xd, twin)
    at = (h, (h + 3) % 4, (h + 1) % 4, (h + 2) % 4)

    sends = []
    recv_index = {}

    def recv_sem(name):
        return recv_sems.at[recv_index.setdefault(name, len(recv_index))]

    def send(src, dst, name, to):
        copy = pltpu.make_async_remote_copy(
            src_ref=src, dst_ref=dst, send_sem=send_sems.at[len(sends)], recv_sem=recv_sem(name),
            device_id=to, device_id_type=MESH,
        )
        copy.start()
        sends.append(copy)

    def arrived(dst, name):
        pltpu.make_async_remote_copy(
            src_ref=dst, dst_ref=dst, send_sem=send_sems.at[0], recv_sem=recv_sem(name),
            device_id=twin, device_id_type=MESH,
        ).wait_recv()

    barrier = pltpu.get_barrier_semaphore()
    for partner in partners:
        pl.semaphore_signal(barrier, inc=1, device_id=partner, device_id_type=MESH)
    own_k = pltpu.make_async_copy(keys_hbm.at[0], kbuf.at[0, h], local_sems.at[0])
    own_v = pltpu.make_async_copy(values_hbm.at[0], vbuf.at[0, h], local_sems.at[1])
    piece = pl.multiple_of(x * 32 + core * 16, 16)
    w_own = w_hbm.at[pl.ds(piece, 16), :]
    own_w = pltpu.make_async_copy(w_own, wbuf.at[c, pl.ds(piece, 16), :], local_sems.at[2])
    own_k.start()
    own_v.start()
    own_w.start()
    pl.semaphore_wait(barrier, len(partners))

    k_own, v_own = keys_hbm.at[0], values_hbm.at[0]

    def w_at(shard, half=None):
        if half is None:
            return wbuf.at[shard, pl.ds(piece, 16), :]
        return wbuf.at[shard, pl.ds(piece, 16), pl.ds(half * 512, 512)]

    send(w_own, w_at(c), "wz-left", zr)
    send(w_own, w_at(c), "wz-right", zl)
    send(k_own, kbuf.at[0, h], ("k", 0, LEFT), zr)
    send(k_own, kbuf.at[0, h], ("k", 0, RIGHT), zl)
    send(k_own, kbuf.at[1, h], ("k", 1, OWN), yu)
    send(v_own, vbuf.at[1, h], ("v", 1, OWN), yu)
    send(v_own, vtransit.at[h], ("t", OWN), yd)

    for head in range(HQ):
        q_s[head // PER, (head % PER) * TOK:(head % PER + 1) * TOK, :] = (
            queries[:, head * HD:(head + 1) * HD]
        )
    line = segs[...]
    mine = jnp.zeros((1, TOK), jnp.int32)
    for slab in range(16):
        mine = jnp.where(c == slab, line[:, slab * TOK:(slab + 1) * TOK], mine)
    start = jnp.zeros((1, TOK), jnp.int32)
    for doc in range(1, 8):
        count = jnp.sum((line < doc).astype(jnp.int32), axis=1, keepdims=True)
        start = jnp.where(mine == doc, count, start)
    start_s[...] = jnp.concatenate([start] * PER, axis=1)
    qpos = c * TOK + lax.broadcasted_iota(jnp.int32, (1, TOK), 1)
    qpos_s[...] = jnp.concatenate([qpos] * PER, axis=1)

    def attend(r, hh, diagonal):
        first = ((y - r) * 4 + hh) * TOK

        def block(b, carry):
            lane = pl.multiple_of((b // (BLOCKS // KVH)) * HD, HD)
            k = kbuf[r, hh, :, pl.ds(lane, HD)]
            v = vbuf[r, hh, :, pl.ds(lane, HD)]
            s = lax.dot_general(
                k, q_s[b], (((1,), (1,)), ((), ())), preferred_element_type=jnp.float32
            )
            kpos = first + lax.broadcasted_iota(jnp.int32, (TOK, LANES), 0)
            ok = kpos >= start_s[...]
            if diagonal:
                ok = ok & (kpos <= qpos_s[...])
            s = jnp.where(ok, s, NEG)
            top = jnp.max(s, axis=0, keepdims=True)
            if diagonal:
                m = top
            else:
                old = m_s[b]
                m = jnp.maximum(old, top)
                alpha = jnp.exp2((old - m) * SCALE2)
            p = jnp.exp2((s - m) * SCALE2)
            total = jnp.sum(p, axis=0, keepdims=True)
            mixed = lax.dot_general(
                v, p.astype(jnp.bfloat16), (((0,), (0,)), ((), ())),
                preferred_element_type=jnp.float32,
            )
            m_s[b] = m
            if diagonal:
                l_s[b] = total
                acc_s[b] = mixed
            else:
                l_s[b] = l_s[b] * alpha + total
                acc_s[b] = acc_s[b] * alpha + mixed
            return carry

        lax.fori_loop(0, BLOCKS, block, 0)

    def same_row(g):
        hh = at[g]
        arrived(kbuf.at[0, hh], ("k", 0, g))
        if g == LEFT:
            send(kbuf.at[0, hh], kbuf.at[0, hh], ("k", 0, FAR), zr)
        send(kbuf.at[0, hh], kbuf.at[1, hh], ("k", 1, g), yu)
        arrived(vbuf.at[0, hh], ("v", 0, g))
        if g == RIGHT:
            send(vbuf.at[0, hh], vbuf.at[0, hh], ("v", 0, FAR), zl)
        send(vbuf.at[0, hh], vbuf.at[1, hh], ("v", 1, g), yu)
        send(vbuf.at[0, hh], vtransit.at[hh], ("t", g), yd)

        @pl.when(hh < h)
        def _():
            attend(0, hh, False)

    def next_row(g):
        hh = at[g]
        arrived(kbuf.at[1, hh], ("k", 1, g))
        send(kbuf.at[1, hh], kbuf.at[2, hh], ("k", 2, g), yu)
        arrived(vtransit.at[hh], ("t", g))
        send(vtransit.at[hh], vbuf.at[2, hh], ("v", 2, g), yd)
        arrived(vbuf.at[1, hh], ("v", 1, g))

        @pl.when(y >= 1)
        def _():
            attend(1, hh, False)

    def last_row(g):
        hh = at[g]
        arrived(kbuf.at[2, hh], ("k", 2, g))
        arrived(vbuf.at[2, hh], ("v", 2, g))

        @pl.when((y >= 2) & (hh >= h))
        def _():
            attend(2, hh, False)

    left, right = y * 4 + at[LEFT], y * 4 + at[RIGHT]
    far = y * 4 + at[FAR]
    arrived(w_at(left), "wz-left")
    send(w_at(left, 0), w_at(left, 0), "wz-far-0", zr)
    arrived(w_at(right), "wz-right")
    send(w_at(right, 1), w_at(right, 1), "wz-far-1", zl)
    send(v_own, vbuf.at[0, h], ("v", 0, LEFT), zr)
    send(v_own, vbuf.at[0, h], ("v", 0, RIGHT), zl)

    own_k.wait()
    own_v.wait()
    own_w.wait()
    attend(0, h, True)
    next_row(OWN)

    def w_row(row, half=None):
        if half is None:
            return wbuf.at[pl.ds(row * 4, 4), pl.ds(piece, 16), :]
        return wbuf.at[pl.ds(row * 4, 4), pl.ds(piece, 16), pl.ds(half * 512, 512)]

    arrived(w_at(far, 0), "wz-far-0")
    arrived(w_at(far, 1), "wz-far-1")
    send(w_row(y), w_row(y), "wy-down", yu)
    send(w_row(y), w_row(y), "wy-up", yd)
    last_row(OWN)
    below, above = (y + 3) % 4, (y + 1) % 4
    across = (y + 2) % 4
    arrived(w_row(below), "wy-down")
    send(w_row(below, 0), w_row(below, 0), "wy-far-0", yu)
    arrived(w_row(above), "wy-up")
    send(w_row(above, 1), w_row(above, 1), "wy-far-1", yd)
    arrived(w_row(across, 0), "wy-far-0")
    arrived(w_row(across, 1), "wy-far-1")

    def w_x(xx, half=None):
        rows = pl.ds(pl.multiple_of(xx * 32 + core * 16, 16), 16)
        if half is None:
            return wbuf.at[:, rows, :]
        return wbuf.at[pl.ds(half * 8, 8), rows, :]

    def w_twin(xx):
        return wbuf.at[:, pl.ds(pl.multiple_of(xx * 32 + (1 - core) * 16, 16), 16), :]

    xb, xa, xo = (x + 3) % 4, (x + 1) % 4, (x + 2) % 4
    send(w_x(x), w_x(x), "wx-down", xu)
    send(w_x(x), w_x(x), "wx-up", xd)
    send(w_x(x), w_x(x), "wc-own", twin)

    same_row(LEFT)
    same_row(RIGHT)
    next_row(LEFT)
    next_row(RIGHT)
    arrived(w_x(xb), "wx-down")
    send(w_x(xb, 0), w_x(xb, 0), "wx-far-0", xu)
    send(w_x(xb), w_x(xb), "wc-down", twin)
    arrived(w_x(xa), "wx-up")
    send(w_x(xa, 1), w_x(xa, 1), "wx-far-1", xd)
    send(w_x(xa), w_x(xa), "wc-up", twin)
    same_row(FAR)
    last_row(LEFT)
    last_row(RIGHT)
    next_row(FAR)
    arrived(w_x(xo, 0), "wx-far-0")
    arrived(w_x(xo, 1), "wx-far-1")
    send(w_x(xo), w_x(xo), "wc-far", twin)
    last_row(FAR)

    for head in range(HQ):
        b, part = head // PER, (head % PER) * TOK
        mixed = acc_s[b, :, part:part + TOK] / l_s[b, :, part:part + TOK]
        att_s[:, head * HD:(head + 1) * HD] = mixed.T.astype(jnp.bfloat16)
    arrived(w_twin(x), "wc-own")
    arrived(w_twin(xb), "wc-down")
    arrived(w_twin(xa), "wc-up")
    arrived(w_twin(xo), "wc-far")

    def project(n, carry):
        cols = pl.ds(pl.multiple_of(n * 256, 256), 256)
        weight = wbuf[:, :, cols].reshape(HQ * HD, 256)
        hidden_out[:, cols] = residual[:, cols].astype(jnp.float32) + jnp.dot(
            att_s[...], weight, preferred_element_type=jnp.float32
        )
        return carry

    lax.fori_loop(0, WIDTH // 256, project, 0)
    hidden = hidden_out[...]
    mean = jnp.mean(hidden * hidden, axis=1, keepdims=True)
    normed = (hidden * lax.rsqrt(mean + 1e-06) * gain[...]).astype(jnp.bfloat16)

    owner = lax.broadcasted_iota(jnp.int32, (OWNERS, TOK), 0)
    hit = jnp.zeros((OWNERS, TOK), jnp.float32)
    mix = jnp.zeros((OWNERS, TOK), jnp.float32)
    for k in range(TOP):
        match = owner == ids[k:k + 1, :]
        hit = jnp.where(match, 1.0, hit)
        mix = jnp.where(match, weights[k:k + 1, :], mix)
    earlier = lax.broadcasted_iota(jnp.int32, (TOK, TOK), 0) < lax.broadcasted_iota(
        jnp.int32, (TOK, TOK), 1
    )
    rank = jnp.dot(
        hit.astype(jnp.bfloat16), jnp.where(earlier, 1.0, 0.0).astype(jnp.bfloat16),
        preferred_element_type=jnp.float32,
    )
    slot = lax.broadcasted_iota(jnp.int32, (CAP, TOK), 0).astype(jnp.float32)
    places, mixes = [], []
    for owner_index in range(OWNERS):
        one = slice(owner_index, owner_index + 1)
        here = (rank[one] == slot) & (hit[one] > 0.5)
        places.append(jnp.where(here, 1.0, 0.0))
        mixes.append(jnp.where(here, mix[one], 0.0))
    place = jnp.concatenate(places, axis=0).astype(jnp.bfloat16)
    rows_out[...] = jnp.dot(place, normed, preferred_element_type=jnp.float32).astype(jnp.bfloat16)
    mixed = jnp.concatenate(mixes, axis=0)
    high = mixed.astype(jnp.bfloat16)
    hi_out[...] = high
    lo_out[...] = (mixed - high.astype(jnp.float32)).astype(jnp.bfloat16)

    for copy in sends:
        copy.wait_send()


def attend_call(queries, segments, residual, gain, ids, weights, keys, values, out_weight):
    vmem = pl.BlockSpec(memory_space=pltpu.VMEM)
    hbm = pl.BlockSpec(memory_space=pl.ANY)
    return pl.pallas_call(
        attend_kernel,
        out_shape=(
            jax.ShapeDtypeStruct((TOK, WIDTH), jnp.float32),
            jax.ShapeDtypeStruct((SLOTS, WIDTH), jnp.bfloat16),
            jax.ShapeDtypeStruct((SLOTS, TOK), jnp.bfloat16),
            jax.ShapeDtypeStruct((SLOTS, TOK), jnp.bfloat16),
        ),
        in_specs=[vmem] * 6 + [hbm] * 3,
        out_specs=(vmem,) * 4,
        scratch_shapes=[
            pltpu.VMEM((3, 4, TOK, KVH * HD), jnp.bfloat16),
            pltpu.VMEM((3, 4, TOK, KVH * HD), jnp.bfloat16),
            pltpu.VMEM((4, TOK, KVH * HD), jnp.bfloat16),
            pltpu.VMEM((HQ, HD, WIDTH), jnp.bfloat16),
            pltpu.VMEM((BLOCKS, LANES, HD), jnp.bfloat16),
            pltpu.VMEM((BLOCKS, 1, LANES), jnp.float32),
            pltpu.VMEM((BLOCKS, 1, LANES), jnp.float32),
            pltpu.VMEM((BLOCKS, HD, LANES), jnp.float32),
            pltpu.VMEM((1, LANES), jnp.int32),
            pltpu.VMEM((1, LANES), jnp.int32),
            pltpu.VMEM((TOK, HQ * HD), jnp.bfloat16),
            pltpu.SemaphoreType.DMA((48,)),
            pltpu.SemaphoreType.DMA((48,)),
            pltpu.SemaphoreType.DMA((3,)),
        ],
        compiler_params=pltpu.CompilerParams(
            collective_id=0, has_side_effects=True, vmem_limit_bytes=48 << 20
        ),
    )(queries, segments, residual, gain, ids, weights, keys, values, out_weight)


def per_device(
    queries, keys, values, segments, residual, out_weight, gain, expert_ids, route_weights,
    w_gate, w_up, w_down,
):
    hidden, rows, high, low = attend_call(
        queries[0],
        segments,
        residual[0],
        gain[None],
        expert_ids[0].T,
        route_weights[0].T,
        keys,
        values,
        out_weight,
    )
    outgoing = rows.reshape(OWNERS, CAP, WIDTH)
    arrived = lax.all_to_all(outgoing, "exp", split_axis=0, concat_axis=0, tiled=True)
    flat_rows = arrived.reshape(SLOTS, WIDTH)
    gate_part = jnp.dot(flat_rows, w_gate[0], preferred_element_type=jnp.float32)
    up_part = jnp.dot(flat_rows, w_up[0], preferred_element_type=jnp.float32)
    expert_hidden = (jax.nn.silu(gate_part) * up_part).astype(jnp.bfloat16)
    expert_out = jnp.dot(expert_hidden, w_down[0], preferred_element_type=jnp.float32).astype(
        jnp.bfloat16
    )
    returned = lax.all_to_all(
        expert_out.reshape(OWNERS, CAP, WIDTH), "exp", split_axis=0, concat_axis=0, tiled=True
    ).reshape(SLOTS, WIDTH)
    moe_sum = lax.dot_general(
        high, returned, (((0,), (0,)), ((), ())), preferred_element_type=jnp.float32
    ) + lax.dot_general(
        low, returned, (((0,), (0,)), ((), ())), preferred_element_type=jnp.float32
    )
    return (hidden + moe_sum).astype(jnp.bfloat16)[None]


def solution(mesh):
    return jax.shard_map(
        per_device,
        mesh=mesh,
        in_specs=(
            P(("dp", "exp"), "ctx", None),
            P(("dp", "exp"), "ctx", None),
            P(("dp", "exp"), "ctx", None),
            P(("dp", "exp"), None),
            P(("dp", "exp"), "ctx", None),
            P("ctx", None),
            P(),
            P(("dp", "exp"), "ctx", None),
            P(("dp", "exp"), "ctx", None),
            P("exp", None, None),
            P("exp", None, None),
            P("exp", None, None),
        ),
        out_specs=P(("dp", "exp"), "ctx", None),
        check_vma=False,
    )
```

```python
import math

import jax
import jax.numpy as jnp
from jax import lax
from jax.experimental import pallas as pl
from jax.experimental.pallas import tpu as pltpu
from jax.sharding import PartitionSpec as P

HQ = 16
KVH = 2
HD = 128
TOP = 8
CAP = 24
TOK = 192
WIDTH = 1024
FFE = 384
OWNERS = 16
SLOTS = OWNERS * CAP
PER = 4
BLOCKS = HQ // PER
LANES = PER * TOK
NEG = -1e30
MESH = pl.DeviceIdType.MESH
SCALE2 = math.log2(math.e) / math.sqrt(HD)
OWN, LEFT, RIGHT, FAR = range(4)


def layer_kernel(
    queries_hbm, segs_hbm, residual_hbm, gain_hbm, ids_hbm, weights_hbm, keys_hbm, values_hbm,
    w_hbm, gate_hbm, up_hbm, down_hbm,
    layer_out,
    segs, residual, gain, ids, weights, gate_up, down,
    kbuf, vbuf, vtransit, wbuf, q_s, m_s, l_s, acc_s, start_s, qpos_s, att_s,
    hidden_s, place_s, mix_s, rows_s, inbox, outbox, back,
    send_sems, recv_sems, local_sems,
):
    c = lax.axis_index("ctx")
    e = lax.axis_index("exp")
    core = lax.axis_index("dp")
    y, h = c // 4, c % 4
    x, z = e // 4, e % 4
    zr, zl = {"ctx": y * 4 + (h + 1) % 4}, {"ctx": y * 4 + (h + 3) % 4}
    yu, yd = {"ctx": ((y + 1) % 4) * 4 + h}, {"ctx": ((y + 3) % 4) * 4 + h}
    xu, xd = {"exp": ((x + 1) % 4) * 4 + z}, {"exp": ((x + 3) % 4) * 4 + z}
    twin = {"dp": 1 - core}
    mates = (z, z + 1 - 2 * (z % 2), (z + 2) % 4, 3 - z)
    peers = [(b, dx) for b in range(4) for dx in (0, 1, 3, 2)]

    def peer(b, dx):
        return ((x + dx) % 4) * 4 + mates[b]

    partners = (zr, zl, yu, yd, twin) + tuple({"exp": peer(*p)} for p in peers if p != (0, 0))
    at = (h, (h + 3) % 4, (h + 1) % 4, (h + 2) % 4)

    sends = []
    recv_index = {}

    def recv_sem(name):
        return recv_sems.at[recv_index.setdefault(name, len(recv_index))]

    def send(src, dst, name, to):
        copy = pltpu.make_async_remote_copy(
            src_ref=src, dst_ref=dst, send_sem=send_sems.at[len(sends)], recv_sem=recv_sem(name),
            device_id=to, device_id_type=MESH,
        )
        copy.start()
        sends.append(copy)

    def arrived(dst, name):
        pltpu.make_async_remote_copy(
            src_ref=dst, dst_ref=dst, send_sem=send_sems.at[0], recv_sem=recv_sem(name),
            device_id=twin, device_id_type=MESH,
        ).wait_recv()

    barrier = pltpu.get_barrier_semaphore()
    for partner in partners:
        pl.semaphore_signal(barrier, inc=1, device_id=partner, device_id_type=MESH)
    own_k = pltpu.make_async_copy(keys_hbm.at[0], kbuf.at[0, h], local_sems.at[0])
    own_v = pltpu.make_async_copy(values_hbm.at[0], vbuf.at[0, h], local_sems.at[1])
    piece = pl.multiple_of(x * 32 + core * 16, 16)
    w_own = w_hbm.at[pl.ds(piece, 16), :]
    own_w = pltpu.make_async_copy(w_own, wbuf.at[c, pl.ds(piece, 16), :], local_sems.at[2])
    loads = [
        pltpu.make_async_copy(
            queries_hbm.at[0, :, pl.ds(head * HD, HD)],
            q_s.at[head // PER, pl.ds((head % PER) * TOK, TOK), :],
            local_sems.at[3 + head],
        )
        for head in range(HQ)
    ]
    loads += [
        pltpu.make_async_copy(src, dst, local_sems.at[3 + HQ + i])
        for i, (src, dst) in enumerate((
            (segs_hbm, segs),
            (ids_hbm, ids),
            (weights_hbm, weights),
        ))
    ]
    late = [
        pltpu.make_async_copy(src, dst, local_sems.at[6 + HQ + i])
        for i, (src, dst) in enumerate((
            (residual_hbm.at[0], residual),
            (gain_hbm, gain),
            (gate_hbm.at[0], gate_up.at[:, pl.ds(0, FFE)]),
            (up_hbm.at[0], gate_up.at[:, pl.ds(FFE, FFE)]),
            (down_hbm.at[0], down),
        ))
    ]
    own_w.start()
    own_k.start()
    own_v.start()
    for load in loads:
        load.start()
    pl.semaphore_wait(barrier, len(partners))

    k_own, v_own = keys_hbm.at[0], values_hbm.at[0]

    def w_at(shard, half=None):
        if half is None:
            return wbuf.at[shard, pl.ds(piece, 16), :]
        return wbuf.at[shard, pl.ds(piece, 16), pl.ds(half * 512, 512)]

    send(w_own, w_at(c), "wz-left", zr)
    send(w_own, w_at(c), "wz-right", zl)
    send(k_own, kbuf.at[0, h], ("k", 0, LEFT), zr)
    send(k_own, kbuf.at[0, h], ("k", 0, RIGHT), zl)
    send(k_own, kbuf.at[1, h], ("k", 1, OWN), yu)
    send(v_own, vbuf.at[1, h], ("v", 1, OWN), yu)
    send(v_own, vtransit.at[h], ("t", OWN), yd)

    for load in late:
        load.start()
    for load in loads:
        load.wait()
    line = segs[...]
    mine = jnp.zeros((1, TOK), jnp.int32)
    for slab in range(16):
        mine = jnp.where(c == slab, line[:, slab * TOK:(slab + 1) * TOK], mine)
    start = jnp.zeros((1, TOK), jnp.int32)
    for doc in range(1, 8):
        count = jnp.sum((line < doc).astype(jnp.int32), axis=1, keepdims=True)
        start = jnp.where(mine == doc, count, start)
    start_s[...] = jnp.concatenate([start] * PER, axis=1)
    qpos = c * TOK + lax.broadcasted_iota(jnp.int32, (1, TOK), 1)
    qpos_s[...] = jnp.concatenate([qpos] * PER, axis=1)

    owner = lax.broadcasted_iota(jnp.int32, (OWNERS, TOK), 0)
    hit = jnp.zeros((OWNERS, TOK), jnp.float32)
    mix = jnp.zeros((OWNERS, TOK), jnp.float32)
    for k in range(TOP):
        match = owner == ids[k:k + 1, :]
        hit = jnp.where(match, 1.0, hit)
        mix = jnp.where(match, weights[k:k + 1, :], mix)
    earlier = lax.broadcasted_iota(jnp.int32, (TOK, TOK), 0) < lax.broadcasted_iota(
        jnp.int32, (TOK, TOK), 1
    )
    rank = jnp.dot(
        hit.astype(jnp.bfloat16), jnp.where(earlier, 1.0, 0.0).astype(jnp.bfloat16),
        preferred_element_type=jnp.float32,
    )
    slot = lax.broadcasted_iota(jnp.int32, (CAP, TOK), 0).astype(jnp.float32)
    places, mixes = [], []
    for owner_index in range(OWNERS):
        one = slice(owner_index, owner_index + 1)
        here = (rank[one] == slot) & (hit[one] > 0.5)
        places.append(jnp.where(here, 1.0, 0.0))
        mixes.append(jnp.where(here, mix[one], 0.0))
    place_s[...] = jnp.concatenate(places, axis=0).astype(jnp.bfloat16)
    mix_s[...] = jnp.concatenate(mixes, axis=0).reshape(OWNERS, CAP, TOK)

    def attend(r, hh, diagonal):
        first = ((y - r) * 4 + hh) * TOK

        def block(b, carry):
            lane = pl.multiple_of((b // (BLOCKS // KVH)) * HD, HD)
            k = kbuf[r, hh, :, pl.ds(lane, HD)]
            v = vbuf[r, hh, :, pl.ds(lane, HD)]
            s = lax.dot_general(
                k, q_s[b], (((1,), (1,)), ((), ())), preferred_element_type=jnp.float32
            )
            kpos = first + lax.broadcasted_iota(jnp.int32, (TOK, LANES), 0)
            ok = kpos >= start_s[...]
            if diagonal:
                ok = ok & (kpos <= qpos_s[...])
            s = jnp.where(ok, s, NEG)
            top = jnp.max(s, axis=0, keepdims=True)
            if diagonal:
                m = top
            else:
                old = m_s[b]
                m = jnp.maximum(old, top)
                alpha = jnp.exp2((old - m) * SCALE2)
            p = jnp.exp2((s - m) * SCALE2)
            total = jnp.sum(p, axis=0, keepdims=True)
            mixed = lax.dot_general(
                v, p.astype(jnp.bfloat16), (((0,), (0,)), ((), ())),
                preferred_element_type=jnp.float32,
            )
            m_s[b] = m
            if diagonal:
                l_s[b] = total
                acc_s[b] = mixed
            else:
                l_s[b] = l_s[b] * alpha + total
                acc_s[b] = acc_s[b] * alpha + mixed
            return carry

        lax.fori_loop(0, BLOCKS, block, 0)

    def same_row(g):
        hh = at[g]
        arrived(kbuf.at[0, hh], ("k", 0, g))
        if g == LEFT:
            send(kbuf.at[0, hh], kbuf.at[0, hh], ("k", 0, FAR), zr)
        send(kbuf.at[0, hh], kbuf.at[1, hh], ("k", 1, g), yu)
        arrived(vbuf.at[0, hh], ("v", 0, g))
        if g == RIGHT:
            send(vbuf.at[0, hh], vbuf.at[0, hh], ("v", 0, FAR), zl)
        send(vbuf.at[0, hh], vbuf.at[1, hh], ("v", 1, g), yu)
        send(vbuf.at[0, hh], vtransit.at[hh], ("t", g), yd)

        @pl.when(hh < h)
        def _():
            attend(0, hh, False)

    def next_row(g):
        hh = at[g]
        arrived(kbuf.at[1, hh], ("k", 1, g))
        send(kbuf.at[1, hh], kbuf.at[2, hh], ("k", 2, g), yu)
        arrived(vtransit.at[hh], ("t", g))
        send(vtransit.at[hh], vbuf.at[2, hh], ("v", 2, g), yd)
        arrived(vbuf.at[1, hh], ("v", 1, g))

        @pl.when(y >= 1)
        def _():
            attend(1, hh, False)

    def last_row(g):
        hh = at[g]
        arrived(kbuf.at[2, hh], ("k", 2, g))
        arrived(vbuf.at[2, hh], ("v", 2, g))

        @pl.when((y >= 2) & (hh >= h))
        def _():
            attend(2, hh, False)

    left, right = y * 4 + at[LEFT], y * 4 + at[RIGHT]
    far = y * 4 + at[FAR]
    arrived(w_at(left), "wz-left")
    send(w_at(left, 0), w_at(left, 0), "wz-far-0", zr)
    arrived(w_at(right), "wz-right")
    send(w_at(right, 1), w_at(right, 1), "wz-far-1", zl)
    send(v_own, vbuf.at[0, h], ("v", 0, LEFT), zr)
    send(v_own, vbuf.at[0, h], ("v", 0, RIGHT), zl)

    own_k.wait()
    own_v.wait()
    own_w.wait()
    attend(0, h, True)
    next_row(OWN)

    def w_row(row, half=None):
        if half is None:
            return wbuf.at[pl.ds(row * 4, 4), pl.ds(piece, 16), :]
        return wbuf.at[pl.ds(row * 4, 4), pl.ds(piece, 16), pl.ds(half * 512, 512)]

    arrived(w_at(far, 0), "wz-far-0")
    arrived(w_at(far, 1), "wz-far-1")
    send(w_row(y), w_row(y), "wy-down", yu)
    send(w_row(y), w_row(y), "wy-up", yd)
    last_row(OWN)
    below, above = (y + 3) % 4, (y + 1) % 4
    across = (y + 2) % 4
    arrived(w_row(below), "wy-down")
    send(w_row(below, 0), w_row(below, 0), "wy-far-0", yu)
    arrived(w_row(above), "wy-up")
    send(w_row(above, 1), w_row(above, 1), "wy-far-1", yd)
    arrived(w_row(across, 0), "wy-far-0")
    arrived(w_row(across, 1), "wy-far-1")

    def w_x(xx, half=None):
        rows = pl.ds(pl.multiple_of(xx * 32 + core * 16, 16), 16)
        if half is None:
            return wbuf.at[:, rows, :]
        return wbuf.at[pl.ds(half * 8, 8), rows, :]

    def w_twin(xx):
        return wbuf.at[:, pl.ds(pl.multiple_of(xx * 32 + (1 - core) * 16, 16), 16), :]

    xb, xa, xo = (x + 3) % 4, (x + 1) % 4, (x + 2) % 4
    send(w_x(x), w_x(x), "wx-down", xu)
    send(w_x(x), w_x(x), "wx-up", xd)
    send(w_x(x), w_x(x), "wc-own", twin)

    same_row(LEFT)
    same_row(RIGHT)
    next_row(LEFT)
    next_row(RIGHT)
    arrived(w_x(xb), "wx-down")
    send(w_x(xb, 0), w_x(xb, 0), "wx-far-0", xu)
    send(w_x(xb), w_x(xb), "wc-down", twin)
    arrived(w_x(xa), "wx-up")
    send(w_x(xa, 1), w_x(xa, 1), "wx-far-1", xd)
    send(w_x(xa), w_x(xa), "wc-up", twin)
    same_row(FAR)
    last_row(LEFT)
    last_row(RIGHT)
    next_row(FAR)
    arrived(w_x(xo, 0), "wx-far-0")
    arrived(w_x(xo, 1), "wx-far-1")
    send(w_x(xo), w_x(xo), "wc-far", twin)
    last_row(FAR)

    for head in range(HQ):
        b, part = head // PER, (head % PER) * TOK
        mixed = acc_s[b, :, part:part + TOK] / l_s[b, :, part:part + TOK]
        att_s[:, head * HD:(head + 1) * HD] = mixed.T.astype(jnp.bfloat16)
    arrived(w_twin(x), "wc-own")
    arrived(w_twin(xb), "wc-down")
    arrived(w_twin(xa), "wc-up")
    arrived(w_twin(xo), "wc-far")

    for load in late:
        load.wait()

    def project(n, carry):
        cols = pl.ds(pl.multiple_of(n * 256, 256), 256)
        weight = wbuf[:, :, cols].reshape(HQ * HD, 256)
        hidden_s[:, cols] = residual[:, cols].astype(jnp.float32) + jnp.dot(
            att_s[...], weight, preferred_element_type=jnp.float32
        )
        return carry

    lax.fori_loop(0, WIDTH // 256, project, 0)
    hidden = hidden_s[...]
    mean = jnp.mean(hidden * hidden, axis=1, keepdims=True)
    normed = (hidden * lax.rsqrt(mean + 1e-06) * gain[...]).astype(jnp.bfloat16)

    placed = jnp.dot(place_s[...], normed, preferred_element_type=jnp.float32)
    rows_s[...] = placed.reshape(OWNERS, CAP, WIDTH).astype(jnp.bfloat16)
    for b, dx in peers:
        if (b, dx) == (0, 0):
            inbox[e] = rows_s[e]
        else:
            to = peer(b, dx)
            send(rows_s.at[to], inbox.at[e], ("out", b, (4 - dx) % 4), {"exp": to})

    def four(ref, b):
        return jnp.concatenate(
            [ref[peer(b, dx)].astype(jnp.float32) for dx in range(4)], axis=0
        )

    for b in range(4):
        for dx in range(4):
            if (b, dx) != (0, 0):
                arrived(inbox.at[peer(b, dx)], ("out", b, dx))
        fed = jnp.dot(
            four(inbox, b).astype(jnp.bfloat16), gate_up[...], preferred_element_type=jnp.float32
        )
        gated, upped = fed[:, :FFE], fed[:, FFE:]
        inner = (gated / (1.0 + jnp.exp(-gated)) * upped).astype(jnp.bfloat16)
        result = jnp.dot(inner, down[...], preferred_element_type=jnp.float32)
        result = result.reshape(4, CAP, WIDTH).astype(jnp.bfloat16)
        for dx in range(4):
            if (b, dx) == (0, 0):
                back[e] = result[dx]
            else:
                outbox[peer(b, dx)] = result[dx]
        for dx in (0, 1, 3, 2):
            if (b, dx) != (0, 0):
                to = peer(b, dx)
                send(outbox.at[to], back.at[e], ("back", b, (4 - dx) % 4), {"exp": to})

    for b in range(4):
        for dx in range(4):
            if (b, dx) != (0, 0):
                arrived(back.at[peer(b, dx)], ("back", b, dx))
        mixes = four(mix_s, b)
        high = mixes.astype(jnp.bfloat16)
        low = (mixes - high.astype(jnp.float32)).astype(jnp.bfloat16)
        got = four(back, b).astype(jnp.bfloat16)
        hidden_s[...] += lax.dot_general(
            jnp.concatenate([high, low], axis=0), jnp.concatenate([got, got], axis=0),
            (((0,), (0,)), ((), ())), preferred_element_type=jnp.float32,
        )
    layer_out[...] = hidden_s[...].astype(jnp.bfloat16)

    for copy in sends:
        copy.wait_send()


def per_device(
    queries, keys, values, segments, residual, out_weight, gain, expert_ids, route_weights,
    w_gate, w_up, w_down,
):
    hbm = pl.BlockSpec(memory_space=pl.ANY)
    bf16, f32 = jnp.bfloat16, jnp.float32
    result = pl.pallas_call(
        layer_kernel,
        out_shape=jax.ShapeDtypeStruct((TOK, WIDTH), bf16),
        in_specs=[hbm] * 12,
        out_specs=pl.BlockSpec(memory_space=pltpu.VMEM),
        scratch_shapes=[
            pltpu.VMEM((1, 16 * TOK), jnp.int32),
            pltpu.VMEM((TOK, WIDTH), bf16),
            pltpu.VMEM((1, WIDTH), f32),
            pltpu.VMEM((TOP, TOK), jnp.int32),
            pltpu.VMEM((TOP, TOK), f32),
            pltpu.VMEM((WIDTH, 2 * FFE), bf16),
            pltpu.VMEM((FFE, WIDTH), bf16),
            pltpu.VMEM((3, 4, TOK, KVH * HD), bf16),
            pltpu.VMEM((3, 4, TOK, KVH * HD), bf16),
            pltpu.VMEM((4, TOK, KVH * HD), bf16),
            pltpu.VMEM((HQ, HD, WIDTH), bf16),
            pltpu.VMEM((BLOCKS, LANES, HD), bf16),
            pltpu.VMEM((BLOCKS, 1, LANES), f32),
            pltpu.VMEM((BLOCKS, 1, LANES), f32),
            pltpu.VMEM((BLOCKS, HD, LANES), f32),
            pltpu.VMEM((1, LANES), jnp.int32),
            pltpu.VMEM((1, LANES), jnp.int32),
            pltpu.VMEM((TOK, HQ * HD), bf16),
            pltpu.VMEM((TOK, WIDTH), f32),
            pltpu.VMEM((SLOTS, TOK), bf16),
            pltpu.VMEM((OWNERS, CAP, TOK), f32),
            pltpu.VMEM((OWNERS, CAP, WIDTH), bf16),
            pltpu.VMEM((OWNERS, CAP, WIDTH), bf16),
            pltpu.VMEM((OWNERS, CAP, WIDTH), bf16),
            pltpu.VMEM((OWNERS, CAP, WIDTH), bf16),
            pltpu.SemaphoreType.DMA((80,)),
            pltpu.SemaphoreType.DMA((80,)),
            pltpu.SemaphoreType.DMA((32,)),
        ],
        compiler_params=pltpu.CompilerParams(
            collective_id=0, has_side_effects=True, vmem_limit_bytes=67043328
        ),
    )(
        queries, segments, residual, gain[None], expert_ids[0].T, route_weights[0].T, keys, values,
        out_weight, w_gate, w_up, w_down,
    )
    return result[None]


def solution(mesh):
    return jax.shard_map(
        per_device,
        mesh=mesh,
        in_specs=(
            P(("dp", "exp"), "ctx", None),
            P(("dp", "exp"), "ctx", None),
            P(("dp", "exp"), "ctx", None),
            P(("dp", "exp"), None),
            P(("dp", "exp"), "ctx", None),
            P("ctx", None),
            P(),
            P(("dp", "exp"), "ctx", None),
            P(("dp", "exp"), "ctx", None),
            P("exp", None, None),
            P("exp", None, None),
            P("exp", None, None),
        ),
        out_specs=P(("dp", "exp"), "ctx", None),
        check_vma=False,
    )
```

```python
import math

import jax
import jax.numpy as jnp
from jax import lax
from jax.experimental import pallas as pl
from jax.experimental.pallas import tpu as pltpu
from jax.sharding import PartitionSpec as P

HQ = 16
KVH = 2
HD = 128
TOP = 8
CAP = 24
TOK = 192
WIDTH = 1024
FFE = 384
OWNERS = 16
SLOTS = OWNERS * CAP
PER = 4
BLOCKS = HQ // PER
LANES = PER * TOK
NEG = -1e30
MESH = pl.DeviceIdType.MESH
SCALE2 = math.log2(math.e) / math.sqrt(HD)
OWN, LEFT, RIGHT, FAR = range(4)


def layer_kernel(
    queries_hbm, segs_hbm, residual_hbm, gain_hbm, ids_hbm, weights_hbm, keys_hbm, values_hbm,
    w_hbm, gate_hbm, up_hbm, down_hbm,
    layer_out,
    segs, residual, gain, ids, weights, gate_up, down,
    kbuf, vbuf, vtransit, wbuf, q_s, m_s, l_s, acc_s, start_s, qpos_s, att_s,
    hidden_s, place_s, mix_s, rows_s, inbox, outbox, back,
    send_sems, recv_sems, local_sems,
):
    c = lax.axis_index("ctx")
    e = lax.axis_index("exp")
    core = lax.axis_index("dp")
    y, h = c // 4, c % 4
    x, z = e // 4, e % 4
    zr, zl = {"ctx": y * 4 + (h + 1) % 4}, {"ctx": y * 4 + (h + 3) % 4}
    yu, yd = {"ctx": ((y + 1) % 4) * 4 + h}, {"ctx": ((y + 3) % 4) * 4 + h}
    xu, xd = {"exp": ((x + 1) % 4) * 4 + z}, {"exp": ((x + 3) % 4) * 4 + z}
    twin = {"dp": 1 - core}
    mates = (z, z + 1 - 2 * (z % 2), (z + 2) % 4, 3 - z)
    peers = [(b, dx) for b in range(4) for dx in (0, 1, 3, 2)]

    def peer(b, dx):
        return ((x + dx) % 4) * 4 + mates[b]

    partners = (zr, zl, yu, yd, twin) + tuple({"exp": peer(*p)} for p in peers if p != (0, 0))
    at = (h, (h + 3) % 4, (h + 1) % 4, (h + 2) % 4)

    sends = []
    recv_index = {}

    def recv_sem(name):
        return recv_sems.at[recv_index.setdefault(name, len(recv_index))]

    def send(src, dst, name, to):
        copy = pltpu.make_async_remote_copy(
            src_ref=src, dst_ref=dst, send_sem=send_sems.at[len(sends)], recv_sem=recv_sem(name),
            device_id=to, device_id_type=MESH,
        )
        copy.start()
        sends.append(copy)

    def arrived(dst, name):
        pltpu.make_async_remote_copy(
            src_ref=dst, dst_ref=dst, send_sem=send_sems.at[0], recv_sem=recv_sem(name),
            device_id=twin, device_id_type=MESH,
        ).wait_recv()

    barrier = pltpu.get_barrier_semaphore()
    for partner in partners:
        pl.semaphore_signal(barrier, inc=1, device_id=partner, device_id_type=MESH)
    own_k = pltpu.make_async_copy(keys_hbm.at[0], kbuf.at[0, h], local_sems.at[0])
    own_v = pltpu.make_async_copy(values_hbm.at[0], vbuf.at[0, h], local_sems.at[1])
    piece = pl.multiple_of(x * 32 + core * 16, 16)
    w_own = w_hbm.at[pl.ds(piece, 16), :]
    own_w = pltpu.make_async_copy(w_own, wbuf.at[c, pl.ds(piece, 16), :], local_sems.at[2])
    loads = [
        pltpu.make_async_copy(
            queries_hbm.at[0, :, pl.ds(head * HD, HD)],
            q_s.at[head // PER, pl.ds((head % PER) * TOK, TOK), :],
            local_sems.at[3 + head],
        )
        for head in range(HQ)
    ]
    loads += [
        pltpu.make_async_copy(src, dst, local_sems.at[3 + HQ + i])
        for i, (src, dst) in enumerate((
            (segs_hbm, segs),
            (ids_hbm, ids),
            (weights_hbm, weights),
        ))
    ]
    late = [
        pltpu.make_async_copy(src, dst, local_sems.at[6 + HQ + i])
        for i, (src, dst) in enumerate((
            (residual_hbm.at[0], residual),
            (gain_hbm, gain),
            (gate_hbm.at[0], gate_up.at[:, pl.ds(0, FFE)]),
            (up_hbm.at[0], gate_up.at[:, pl.ds(FFE, FFE)]),
            (down_hbm.at[0], down),
        ))
    ]
    own_w.start()
    own_k.start()
    own_v.start()
    for load in loads:
        load.start()
    pl.semaphore_wait(barrier, len(partners))

    k_own, v_own = keys_hbm.at[0], values_hbm.at[0]

    def w_at(shard, half=None):
        if half is None:
            return wbuf.at[shard, pl.ds(piece, 16), :]
        return wbuf.at[shard, pl.ds(piece, 16), pl.ds(half * 512, 512)]

    send(w_own, w_at(c), "wz-left", zr)
    send(w_own, w_at(c), "wz-right", zl)
    send(k_own, kbuf.at[1, h], ("k", 1, OWN), yu)
    send(v_own, vbuf.at[1, h], ("v", 1, OWN), yu)
    send(v_own, vtransit.at[h], ("t", OWN), yd)

    for load in late:
        load.start()
    for load in loads:
        load.wait()
    line = segs[...]
    mine = jnp.zeros((1, TOK), jnp.int32)
    for slab in range(16):
        mine = jnp.where(c == slab, line[:, slab * TOK:(slab + 1) * TOK], mine)
    start = jnp.zeros((1, TOK), jnp.int32)
    for doc in range(1, 8):
        count = jnp.sum((line < doc).astype(jnp.int32), axis=1, keepdims=True)
        start = jnp.where(mine == doc, count, start)
    start_s[...] = jnp.concatenate([start] * PER, axis=1)
    qpos = c * TOK + lax.broadcasted_iota(jnp.int32, (1, TOK), 1)
    qpos_s[...] = jnp.concatenate([qpos] * PER, axis=1)

    owner = lax.broadcasted_iota(jnp.int32, (OWNERS, TOK), 0)
    hit = jnp.zeros((OWNERS, TOK), jnp.float32)
    mix = jnp.zeros((OWNERS, TOK), jnp.float32)
    for k in range(TOP):
        match = owner == ids[k:k + 1, :]
        hit = jnp.where(match, 1.0, hit)
        mix = jnp.where(match, weights[k:k + 1, :], mix)
    earlier = lax.broadcasted_iota(jnp.int32, (TOK, TOK), 0) < lax.broadcasted_iota(
        jnp.int32, (TOK, TOK), 1
    )
    rank = jnp.dot(
        hit.astype(jnp.bfloat16), jnp.where(earlier, 1.0, 0.0).astype(jnp.bfloat16),
        preferred_element_type=jnp.float32,
    )
    slot = lax.broadcasted_iota(jnp.int32, (CAP, TOK), 0).astype(jnp.float32)
    places, mixes = [], []
    for owner_index in range(OWNERS):
        one = slice(owner_index, owner_index + 1)
        here = (rank[one] == slot) & (hit[one] > 0.5)
        places.append(jnp.where(here, 1.0, 0.0))
        mixes.append(jnp.where(here, mix[one], 0.0))
    place_s[...] = jnp.concatenate(places, axis=0).astype(jnp.bfloat16)
    mix_s[...] = jnp.concatenate(mixes, axis=0).reshape(OWNERS, CAP, TOK)

    def attend(r, hh, diagonal):
        first = ((y - r) * 4 + hh) * TOK

        def block(b, carry):
            lane = pl.multiple_of((b // (BLOCKS // KVH)) * HD, HD)
            k = kbuf[r, hh, :, pl.ds(lane, HD)]
            v = vbuf[r, hh, :, pl.ds(lane, HD)]
            s = lax.dot_general(
                k, q_s[b], (((1,), (1,)), ((), ())), preferred_element_type=jnp.float32
            )
            kpos = first + lax.broadcasted_iota(jnp.int32, (TOK, LANES), 0)
            ok = kpos >= start_s[...]
            if diagonal:
                ok = ok & (kpos <= qpos_s[...])
            s = jnp.where(ok, s, NEG)
            top = jnp.max(s, axis=0, keepdims=True)
            if diagonal:
                m = top
            else:
                old = m_s[b]
                m = jnp.maximum(old, top)
                alpha = jnp.exp2((old - m) * SCALE2)
            p = jnp.exp2((s - m) * SCALE2)
            total = jnp.sum(p, axis=0, keepdims=True)
            mixed = lax.dot_general(
                v, p.astype(jnp.bfloat16), (((0,), (0,)), ((), ())),
                preferred_element_type=jnp.float32,
            )
            m_s[b] = m
            if diagonal:
                l_s[b] = total
                acc_s[b] = mixed
            else:
                l_s[b] = l_s[b] * alpha + total
                acc_s[b] = acc_s[b] * alpha + mixed
            return carry

        lax.fori_loop(0, BLOCKS, block, 0)

    def same_row(g):
        hh = at[g]

        def k_part():
            arrived(kbuf.at[0, hh], ("k", 0, g))
            if g == LEFT:
                send(kbuf.at[0, hh], kbuf.at[0, hh], ("k", 0, FAR), zr)
            send(kbuf.at[0, hh], kbuf.at[1, hh], ("k", 1, g), yu)

        def v_part():
            arrived(vbuf.at[0, hh], ("v", 0, g))
            if g == RIGHT:
                send(vbuf.at[0, hh], vbuf.at[0, hh], ("v", 0, FAR), zl)
            send(vbuf.at[0, hh], vtransit.at[hh], ("t", g), yd)
            send(vbuf.at[0, hh], vbuf.at[1, hh], ("v", 1, g), yu)

        return k_part, v_part

    def same_attend(g):
        hh = at[g]

        @pl.when(hh < h)
        def _():
            attend(0, hh, False)

    def next_row(g):
        hh = at[g]
        arrived(kbuf.at[1, hh], ("k", 1, g))
        send(kbuf.at[1, hh], kbuf.at[2, hh], ("k", 2, g), yu)
        arrived(vtransit.at[hh], ("t", g))
        send(vtransit.at[hh], vbuf.at[2, hh], ("v", 2, g), yd)
        arrived(vbuf.at[1, hh], ("v", 1, g))

        @pl.when(y >= 1)
        def _():
            attend(1, hh, False)

    def last_row(g):
        hh = at[g]
        arrived(kbuf.at[2, hh], ("k", 2, g))
        arrived(vbuf.at[2, hh], ("v", 2, g))

        @pl.when((y >= 2) & (hh >= h))
        def _():
            attend(2, hh, False)

    left, right = y * 4 + at[LEFT], y * 4 + at[RIGHT]
    far = y * 4 + at[FAR]
    arrived(w_at(left), "wz-left")
    send(w_at(left, 0), w_at(left, 0), "wz-far-0", zr)
    arrived(w_at(right), "wz-right")
    send(w_at(right, 1), w_at(right, 1), "wz-far-1", zl)
    send(k_own, kbuf.at[0, h], ("k", 0, LEFT), zr)
    send(v_own, vbuf.at[0, h], ("v", 0, RIGHT), zl)
    send(v_own, vbuf.at[0, h], ("v", 0, LEFT), zr)
    send(k_own, kbuf.at[0, h], ("k", 0, RIGHT), zl)

    own_k.wait()
    own_v.wait()
    own_w.wait()
    attend(0, h, True)
    next_row(OWN)

    def w_row(row, half=None):
        if half is None:
            return wbuf.at[pl.ds(row * 4, 4), pl.ds(piece, 16), :]
        return wbuf.at[pl.ds(row * 4, 4), pl.ds(piece, 16), pl.ds(half * 512, 512)]

    arrived(w_at(far, 0), "wz-far-0")
    arrived(w_at(far, 1), "wz-far-1")
    send(w_row(y), w_row(y), "wy-down", yu)
    send(w_row(y), w_row(y), "wy-up", yd)
    last_row(OWN)
    below, above = (y + 3) % 4, (y + 1) % 4
    across = (y + 2) % 4
    arrived(w_row(below), "wy-down")
    send(w_row(below, 0), w_row(below, 0), "wy-far-0", yu)
    arrived(w_row(above), "wy-up")
    send(w_row(above, 1), w_row(above, 1), "wy-far-1", yd)
    arrived(w_row(across, 0), "wy-far-0")
    arrived(w_row(across, 1), "wy-far-1")

    def w_x(xx, half=None):
        rows = pl.ds(pl.multiple_of(xx * 32 + core * 16, 16), 16)
        if half is None:
            return wbuf.at[:, rows, :]
        return wbuf.at[pl.ds(half * 8, 8), rows, :]

    def w_twin(xx):
        return wbuf.at[:, pl.ds(pl.multiple_of(xx * 32 + (1 - core) * 16, 16), 16), :]

    xb, xa, xo = (x + 3) % 4, (x + 1) % 4, (x + 2) % 4
    send(w_x(x), w_x(x), "wx-down", xu)
    send(w_x(x), w_x(x), "wx-up", xd)
    send(w_x(x), w_x(x), "wc-own", twin)

    left_k, left_v = same_row(LEFT)
    right_k, right_v = same_row(RIGHT)
    left_k()
    right_v()
    left_v()
    right_k()
    same_attend(LEFT)
    same_attend(RIGHT)
    next_row(LEFT)
    next_row(RIGHT)
    arrived(w_x(xb), "wx-down")
    send(w_x(xb, 0), w_x(xb, 0), "wx-far-0", xu)
    send(w_x(xb), w_x(xb), "wc-down", twin)
    arrived(w_x(xa), "wx-up")
    send(w_x(xa, 1), w_x(xa, 1), "wx-far-1", xd)
    send(w_x(xa), w_x(xa), "wc-up", twin)
    far_k, far_v = same_row(FAR)
    far_k()
    far_v()
    same_attend(FAR)
    last_row(LEFT)
    last_row(RIGHT)
    next_row(FAR)
    arrived(w_x(xo, 0), "wx-far-0")
    arrived(w_x(xo, 1), "wx-far-1")
    send(w_x(xo), w_x(xo), "wc-far", twin)
    last_row(FAR)

    for head in range(HQ):
        b, part = head // PER, (head % PER) * TOK
        mixed = acc_s[b, :, part:part + TOK] / l_s[b, :, part:part + TOK]
        att_s[:, head * HD:(head + 1) * HD] = mixed.T.astype(jnp.bfloat16)
    arrived(w_twin(x), "wc-own")
    arrived(w_twin(xb), "wc-down")
    arrived(w_twin(xa), "wc-up")
    arrived(w_twin(xo), "wc-far")

    for load in late:
        load.wait()

    def project(n, carry):
        cols = pl.ds(pl.multiple_of(n * 256, 256), 256)
        weight = wbuf[:, :, cols].reshape(HQ * HD, 256)
        hidden_s[:, cols] = residual[:, cols].astype(jnp.float32) + jnp.dot(
            att_s[...], weight, preferred_element_type=jnp.float32
        )
        return carry

    lax.fori_loop(0, WIDTH // 256, project, 0)
    hidden = hidden_s[...]
    mean = jnp.mean(hidden * hidden, axis=1, keepdims=True)
    normed = (hidden * lax.rsqrt(mean + 1e-06) * gain[...]).astype(jnp.bfloat16)

    placed = jnp.dot(place_s[...], normed, preferred_element_type=jnp.float32)
    rows_s[...] = placed.reshape(OWNERS, CAP, WIDTH).astype(jnp.bfloat16)
    for b, dx in peers:
        if (b, dx) == (0, 0):
            inbox[e] = rows_s[e]
        else:
            to = peer(b, dx)
            send(rows_s.at[to], inbox.at[e], ("out", b, (4 - dx) % 4), {"exp": to})

    def four(ref, b):
        return jnp.concatenate(
            [ref[peer(b, dx)].astype(jnp.float32) for dx in range(4)], axis=0
        )

    for b in range(4):
        for dx in range(4):
            if (b, dx) != (0, 0):
                arrived(inbox.at[peer(b, dx)], ("out", b, dx))
        fed = jnp.dot(
            four(inbox, b).astype(jnp.bfloat16), gate_up[...], preferred_element_type=jnp.float32
        )
        gated, upped = fed[:, :FFE], fed[:, FFE:]
        inner = (gated / (1.0 + jnp.exp(-gated)) * upped).astype(jnp.bfloat16)
        result = jnp.dot(inner, down[...], preferred_element_type=jnp.float32)
        result = result.reshape(4, CAP, WIDTH).astype(jnp.bfloat16)
        for dx in range(4):
            if (b, dx) == (0, 0):
                back[e] = result[dx]
            else:
                outbox[peer(b, dx)] = result[dx]
        for dx in (0, 1, 3, 2):
            if (b, dx) != (0, 0):
                to = peer(b, dx)
                send(outbox.at[to], back.at[e], ("back", b, (4 - dx) % 4), {"exp": to})

    for b in range(4):
        for dx in range(4):
            if (b, dx) != (0, 0):
                arrived(back.at[peer(b, dx)], ("back", b, dx))
        mixes = four(mix_s, b)
        high = mixes.astype(jnp.bfloat16)
        low = (mixes - high.astype(jnp.float32)).astype(jnp.bfloat16)
        got = four(back, b).astype(jnp.bfloat16)
        hidden_s[...] += lax.dot_general(
            jnp.concatenate([high, low], axis=0), jnp.concatenate([got, got], axis=0),
            (((0,), (0,)), ((), ())), preferred_element_type=jnp.float32,
        )
    layer_out[...] = hidden_s[...].astype(jnp.bfloat16)

    for copy in sends:
        copy.wait_send()


def per_device(
    queries, keys, values, segments, residual, out_weight, gain, expert_ids, route_weights,
    w_gate, w_up, w_down,
):
    hbm = pl.BlockSpec(memory_space=pl.ANY)
    bf16, f32 = jnp.bfloat16, jnp.float32
    result = pl.pallas_call(
        layer_kernel,
        out_shape=jax.ShapeDtypeStruct((TOK, WIDTH), bf16),
        in_specs=[hbm] * 12,
        out_specs=pl.BlockSpec(memory_space=pltpu.VMEM),
        scratch_shapes=[
            pltpu.VMEM((1, 16 * TOK), jnp.int32),
            pltpu.VMEM((TOK, WIDTH), bf16),
            pltpu.VMEM((1, WIDTH), f32),
            pltpu.VMEM((TOP, TOK), jnp.int32),
            pltpu.VMEM((TOP, TOK), f32),
            pltpu.VMEM((WIDTH, 2 * FFE), bf16),
            pltpu.VMEM((FFE, WIDTH), bf16),
            pltpu.VMEM((3, 4, TOK, KVH * HD), bf16),
            pltpu.VMEM((3, 4, TOK, KVH * HD), bf16),
            pltpu.VMEM((4, TOK, KVH * HD), bf16),
            pltpu.VMEM((HQ, HD, WIDTH), bf16),
            pltpu.VMEM((BLOCKS, LANES, HD), bf16),
            pltpu.VMEM((BLOCKS, 1, LANES), f32),
            pltpu.VMEM((BLOCKS, 1, LANES), f32),
            pltpu.VMEM((BLOCKS, HD, LANES), f32),
            pltpu.VMEM((1, LANES), jnp.int32),
            pltpu.VMEM((1, LANES), jnp.int32),
            pltpu.VMEM((TOK, HQ * HD), bf16),
            pltpu.VMEM((TOK, WIDTH), f32),
            pltpu.VMEM((SLOTS, TOK), bf16),
            pltpu.VMEM((OWNERS, CAP, TOK), f32),
            pltpu.VMEM((OWNERS, CAP, WIDTH), bf16),
            pltpu.VMEM((OWNERS, CAP, WIDTH), bf16),
            pltpu.VMEM((OWNERS, CAP, WIDTH), bf16),
            pltpu.VMEM((OWNERS, CAP, WIDTH), bf16),
            pltpu.SemaphoreType.DMA((80,)),
            pltpu.SemaphoreType.DMA((80,)),
            pltpu.SemaphoreType.DMA((32,)),
        ],
        compiler_params=pltpu.CompilerParams(
            collective_id=0, has_side_effects=True, vmem_limit_bytes=67043328
        ),
    )(
        queries, segments, residual, gain[None], expert_ids[0].T, route_weights[0].T, keys, values,
        out_weight, w_gate, w_up, w_down,
    )
    return result[None]


def solution(mesh):
    return jax.shard_map(
        per_device,
        mesh=mesh,
        in_specs=(
            P(("dp", "exp"), "ctx", None),
            P(("dp", "exp"), "ctx", None),
            P(("dp", "exp"), "ctx", None),
            P(("dp", "exp"), None),
            P(("dp", "exp"), "ctx", None),
            P("ctx", None),
            P(),
            P(("dp", "exp"), "ctx", None),
            P(("dp", "exp"), "ctx", None),
            P("exp", None, None),
            P("exp", None, None),
            P("exp", None, None),
        ),
        out_specs=P(("dp", "exp"), "ctx", None),
        check_vma=False,
    )
```
